32 devices in a mesh: gx: 4 (over z), gy: 4 (over x, core), gz: 2 (over y).
Axes of the slice: x: 2, y: 2, z: 4, core: 2. Of those that a mesh axis runs over, the one named last changes fastest.
Arguments:
- populations: float32 [19, 32, 32, 256], P(None, 'gx', 'gy', 'gz'), as said below
- solid: int32 [32, 32, 256], P('gx', 'gy', 'gz'), may hold values 0 or 1
- marker_pos: float32 [256, 3, 128], P(('gx', 'gy', 'gz')), may hold values from 2 to 125, as said below
- anchor_offset: float32 [256, 3, 128], P(('gx', 'gy', 'gz')), may hold values from -3 to 3
- links: int32 [256, 2, 128], P(('gx', 'gy', 'gz')), may hold values from 0 to 127
- patch_col: int32 [256, 1], P(('gx', 'gy', 'gz')), may hold values from 0 to 3; in each aligned block of 8 rows (0 to 7, 8 to 15, ...) at most 4 rows name the same one
Outputs:
- new_populations: float32 [19, 32, 32, 256], P(None, 'gx', 'gy', 'gz')
- marker_shift: float32 [256, 3, 128], P(('gx', 'gy', 'gz'))
The draws below stay inside these ranges and needn't reach their ends.
Inputs may be any that keep to these rules, and one draw needn't show every extreme that they name: `marker_pos`: each marker lies from 2 to 5 cells along the first coordinate of its patch, 2 to 5 along the second, 2 to 125 along the third. `patch_col`: among the 8 blocks of one device no patch index is named more than 4 times. `populations`: every population is positive.
All inputs are finite; a program needn't handle non-finite values. No bound on the sum of `solid` on one device may be relied on, other than what follows from the above.
Results may differ from the reference program's by a relative error of at most 0.00035.
Values sent between devices are 32-bit elements; how exact they have to be, the bound alone decides.
A program may use at most 64 MiB of HBM per device.

```python
import math
import jax
import jax.numpy as jnp
import numpy as np

CX = 8
CY = 8
CZ = 128
BLK_DEV = 8
MARK = 128
STEPS = 3
CAP = 4
NX = 32
NY = 32
NZ = 256
NBLK = 256
N_GX = 4
N_GY = 4
N_GZ = 2


WEIGHTS = (1.0 / 3.0,) + (1.0 / 18.0,) * 6 + (1.0 / 36.0,) * 12


def draw_populations(key, part):
    shape = (19, NX, NY, NZ)
    relative = 1.0 + 0.12 * jnp.clip(jax.random.normal(key, shape, jnp.float32), -2.5, 2.5)
    return relative * jnp.array(WEIGHTS, jnp.float32)[:, None, None, None]


def draw_marker_pos(key, part):
    fraction = jax.random.uniform(key, (NBLK, 3, MARK), jnp.float32)
    span = jnp.array([CX - 5, CY - 5, CZ - 5], jnp.float32)[None, :, None]
    return 2.0 + fraction * span


def touch_ends(values, key, smallest, top_value):
    shape = values.shape
    place = [jax.random.randint(jax.random.fold_in(key, axis), (), 0, shape[axis]) for axis in range(len(shape))]
    values = values.at[tuple(place)].set(smallest)
    longest = shape.index(max(shape))
    place[longest] = (place[longest] + 1) % shape[longest]
    return values.at[tuple(place)].set(top_value)


def level_of(stream_key, shape, shards, least, largest):
    factor_of = 1.0
    for position, shards_of in shards:
        steps = jax.random.uniform(jax.random.fold_in(jax.random.fold_in(stream_key, 6), position), (shards_of,), jnp.float32, least / len(shards), largest / len(shards))
        factor_of = factor_of * jnp.repeat(jnp.exp(steps), shape[position] // shards_of).reshape((-1,) + (1,) * (len(shape) - 1 - position))
    return factor_of


def routed_block(stream_key, own, number, rows, amount, top, bound, lean):
    order = jax.random.permutation(stream_key, amount)
    heavy_load, common = portions_of(amount, rows * top, bound, lean, True), portions_of(amount, rows * top, bound, lean, False)
    places = jnp.arange(amount)

    def named(sizes, turn):
        used = int((sizes > 0).sum())
        fixed = max(1, used // 4)
        passed = fixed + (places - fixed + turn * (used - fixed)) % max(1, amount - fixed)
        return jnp.zeros((amount,), jnp.int32).at[order[jnp.where(places < fixed, places, passed)]].set(jnp.asarray(sizes, jnp.int32))

    sizes = jnp.where(number % 4 == 0, named(heavy_load, number // 4), named(common, number - number // 4 - 1))
    mixed = jax.random.permutation(jax.random.fold_in(own, 3), amount)
    giver, taker = mixed[0:amount // 2 * 2:2], mixed[1:amount // 2 * 2:2]
    room = jnp.minimum(sizes[giver] - 1, bound - sizes[taker]) // 2
    room = jnp.where((giver == order[0]) | (taker == order[0]) | (sizes[taker] == 0), 0, jnp.maximum(room, 0))
    passed = jax.random.randint(jax.random.fold_in(own, 4), (amount // 2,), 0, 1 << 20) % (room + 1)
    sizes = sizes.at[giver].add(-passed).at[taker].add(passed)
    members = jnp.searchsorted(jnp.cumsum(sizes), jnp.arange(rows * top), side="right").astype(jnp.int32)
    grid = members.reshape(top, rows).T
    grid = grid[jax.random.permutation(jax.random.fold_in(own, 1), rows)]
    turn = jax.random.randint(jax.random.fold_in(own, 2), (rows, 1), 0, top)
    return jnp.take_along_axis(grid, (jnp.arange(top)[None, :] + turn) % top, axis=1)


def portions_of(amount, total, limit, slope, full):
    portions = [(1 << 20) // math.isqrt(rank ** slope) + 1 for rank in range(1, amount + 1)]
    largest = limit if full else min(limit, max(-(-total // amount), total * portions[0] // sum(portions)))
    least = 1 if total - largest >= amount - 1 else 0
    counts, spare = [largest] + [least] * (amount - 1), total - largest - least * (amount - 1)
    while spare > 0:
        free = [i for i in range(1, amount) if counts[i] < largest] or [i for i in range(1, amount) if counts[i] < limit]
        whole, left = sum([portions[i] for i in free]), spare
        for i in free:
            more = min(limit - counts[i], max(1, left * portions[i] // whole), spare)
            counts[i] = counts[i] + more
            spare = spare - more
    return np.array(counts)


def scatter_about(key, extent, scale, most, shards=(), kind=jnp.bfloat16):
    values = scale * jax.random.normal(key, extent, jnp.float32)
    if shards:
        values = values * level_of(key, extent, shards, -0.22, 0.18)
    return jnp.clip(values, -most, most).astype(kind)


def setup_inputs(seed: int = 0) -> dict:
    streams_of = jax.random.split(jax.random.key(seed), 7)
    populations = draw_populations(jax.random.fold_in(streams_of[6], 71), 0)
    solid = touch_ends((jax.random.randint(streams_of[1], (NX, NY, NZ), 0, 10) < 1).astype(jnp.int32), jax.random.fold_in(streams_of[1], 1), 0, 1)
    marker_pos = draw_marker_pos(jax.random.fold_in(streams_of[6], 71), 0)
    anchor_offset = scatter_about(streams_of[3], (NBLK, 3, MARK), 1.0, 3.0, ((0, 32),), jnp.float32)
    links = touch_ends(jax.random.randint(streams_of[4], (NBLK, 2, MARK), 0, MARK), jax.random.fold_in(streams_of[4], 1), 0, MARK - 1).astype(jnp.int32)
    patch_col_keys = jax.random.split(jax.random.fold_in(streams_of[5], 1), NBLK // BLK_DEV)
    patch_col_turns = jax.random.permutation(jax.random.fold_in(streams_of[5], 3), NBLK // BLK_DEV)
    patch_col = jax.vmap(lambda own, number: routed_block(jax.random.fold_in(streams_of[5], 2), own, number, BLK_DEV, N_GX, 1, CAP, 2))(patch_col_keys, patch_col_turns).reshape((NBLK, 1))
    return dict(populations=populations, solid=solid, marker_pos=marker_pos, anchor_offset=anchor_offset, links=links, patch_col=patch_col)


VELOCITY = ((0, 0, 0), (1, 0, 0), (-1, 0, 0), (0, 1, 0), (0, -1, 0), (0, 0, 1), (0, 0, -1),
            (1, 1, 0), (-1, -1, 0), (1, -1, 0), (-1, 1, 0), (1, 0, 1), (-1, 0, -1), (1, 0, -1), (-1, 0, 1),
            (0, 1, 1), (0, -1, -1), (0, 1, -1), (0, -1, 1))
WEIGHTS = (1.0 / 3.0,) + (1.0 / 18.0,) * 6 + (1.0 / 36.0,) * 12
OPPOSITE = (0, 2, 1, 4, 3, 6, 5, 8, 7, 10, 9, 12, 11, 14, 13, 16, 15, 18, 17)
TAU = 0.8
K_TETHER = 0.05
K_SPRING = 0.1


def project(vector, direction):
    total = None
    for column in range(3):
        if direction[column] != 0:
            term = vector[column] if direction[column] == 1 else -vector[column]
            total = term if total is None else total + term
    if total is None:
        total = jnp.zeros_like(vector[0])
    return total


def moments(parts):
    density = parts[0]
    for number in range(1, 19):
        density = density + parts[number]
    momentum = []
    for column in range(3):
        total = jnp.zeros_like(density)
        for number in range(19):
            sign = VELOCITY[number][column]
            if sign == 1:
                total = total + parts[number]
            elif sign == -1:
                total = total - parts[number]
        momentum.append(total)
    return density, momentum


def collide(parts, field, solid):
    density, momentum = moments(parts)
    speed = [(momentum[column] + 0.5 * field[column]) / density for column in range(3)]
    square = speed[0] * speed[0] + speed[1] * speed[1] + speed[2] * speed[2]
    power = speed[0] * field[0] + speed[1] * field[1] + speed[2] * field[2]
    factor = 1.0 - 0.5 / TAU
    walls = solid == 1
    result = []
    for number in range(19):
        along = project(speed, VELOCITY[number])
        pushed = project(field, VELOCITY[number])
        balance = WEIGHTS[number] * density * (1.0 + 3.0 * along + 4.5 * along * along - 1.5 * square)
        source = factor * WEIGHTS[number] * (3.0 * (pushed - power) + 9.0 * along * pushed)
        post = parts[number] - (parts[number] - balance) / TAU + source
        result.append(jnp.where(walls, parts[OPPOSITE[number]], post))
    return jnp.stack(result)


def marker_force(current, rest, anchor, links):
    total = K_TETHER * (anchor - current)
    for column in range(2):
        chosen = jnp.broadcast_to(links[:, column:column + 1, :], current.shape)
        total = total + K_SPRING * ((jnp.take_along_axis(current, chosen, axis=2) - current)
                                    - (jnp.take_along_axis(rest, chosen, axis=2) - rest))
    return total


def corner_table(current, corners):
    floors = jnp.floor(current)
    base = floors.astype(jnp.int32)
    per_dim = []
    for dim in range(3):
        coord = current[:, dim, :]
        lowest = floors[:, dim, :]
        options = []
        for offset in range(2):
            weight = jnp.maximum(0.0, 1.0 - jnp.abs(coord - (lowest + offset)))
            cell = base[:, dim, :] + offset + corners[dim][:, None]
            options.append((cell.reshape(-1), weight.reshape(-1)))
        per_dim.append(options)
    table = []
    for first in per_dim[0]:
        for second in per_dim[1]:
            for third in per_dim[2]:
                table.append((first[0], second[0], third[0], first[1] * second[1] * third[1]))
    return table


def reference(populations, solid, marker_pos, anchor_offset, links, patch_col):
    blocks = jnp.arange(NBLK, dtype=jnp.int32)
    owner = blocks // BLK_DEV
    corner_x = (patch_col[:, 0] * CX).astype(jnp.int32)
    corner_y = (((owner // N_GZ) % N_GY) * CY).astype(jnp.int32)
    corner_z = ((owner % N_GZ) * CZ).astype(jnp.int32)
    corners = (corner_x, corner_y, corner_z)
    anchor = marker_pos + anchor_offset
    current = marker_pos
    parts = populations
    for repeat in range(STEPS):
        force = marker_force(current, marker_pos, anchor, links)
        table = corner_table(current, corners)
        flat_force = jnp.transpose(force, (1, 0, 2)).reshape(3, -1)
        field = jnp.zeros((3, NX, NY, NZ), jnp.float32)
        for cell_x, cell_y, cell_z, weight in table:
            field = field.at[:, cell_x, cell_y, cell_z].add(flat_force * weight[None, :])
        post = collide(parts, field, solid)
        parts = jnp.stack([jnp.roll(post[number], shift=VELOCITY[number], axis=(0, 1, 2)) for number in range(19)])
        density, momentum = moments(parts)
        velocity = jnp.stack([momentum[column] / density for column in range(3)])
        motion = jnp.zeros((3, NBLK * MARK), jnp.float32)
        for cell_x, cell_y, cell_z, weight in table:
            motion = motion + velocity[:, cell_x, cell_y, cell_z] * weight[None, :]
        current = current + jnp.transpose(motion.reshape(3, NBLK, MARK), (1, 0, 2))
    return parts, current - marker_pos
```

```python
import functools

import jax
import jax.numpy as jnp
from jax import lax
from jax.experimental import pallas as pl
from jax.experimental.pallas import tpu as pltpu
from jax.sharding import PartitionSpec as P

STEPS = 3
VELOCITY = (
    (0, 0, 0), (1, 0, 0), (-1, 0, 0), (0, 1, 0), (0, -1, 0), (0, 0, 1), (0, 0, -1),
    (1, 1, 0), (-1, -1, 0), (1, -1, 0), (-1, 1, 0), (1, 0, 1), (-1, 0, -1), (1, 0, -1),
    (-1, 0, 1), (0, 1, 1), (0, -1, -1), (0, 1, -1), (0, -1, 1),
)
WEIGHTS = (1.0 / 3.0,) + (1.0 / 18.0,) * 6 + (1.0 / 36.0,) * 12
OPPOSITE = (0, 2, 1, 4, 3, 6, 5, 8, 7, 10, 9, 12, 11, 14, 13, 16, 15, 18, 17)
TAU = 0.8
K_TETHER = 0.05
K_SPRING = 0.1
NUMBER = {c: q for q, c in enumerate(VELOCITY)}
ORDER = (
    [q for q in range(19) if VELOCITY[q][0] == 0]
    + [q for q in range(19) if VELOCITY[q][0] == 1]
    + [q for q in range(19) if VELOCITY[q][0] == -1]
)
PLACE = {q: i for i, q in enumerate(ORDER)}
Y_MOVERS = [
    [NUMBER[(0, s, 0)], NUMBER[(1, s, 0)], NUMBER[(-1, s, 0)], NUMBER[(0, s, 1)], NUMBER[(0, s, -1)]]
    for s in (1, -1)
]
Z_MOVERS = [
    [NUMBER[(0, 0, s)], NUMBER[(1, 0, s)], NUMBER[(-1, 0, s)], NUMBER[(0, 1, s)], NUMBER[(0, -1, s)]]
    for s in (1, -1)
]
MESH = pl.DeviceIdType.MESH
PARK = -1000.0
HALF = 64


def axis_sum(values, column):
    total = None
    for q in range(19):
        sign = VELOCITY[q][column]
        if sign == 0:
            continue
        term = values[q]
        total = (term if sign == 1 else -term) if total is None else (
            total + term if sign == 1 else total - term
        )
    return total


def moments(f):
    density = f[0]
    for q in range(1, 19):
        density = density + f[q]
    return density, [axis_sum(f, column) for column in range(3)]


def project(vector, direction):
    total = None
    for column in range(3):
        if direction[column]:
            term = vector[column] if direction[column] == 1 else -vector[column]
            total = term if total is None else total + term
    return total


def collide(f, density, momentum, field, wall):
    over = 1.0 / density
    omega = 1.0 / TAU
    factor = 1.0 - 0.5 / TAU
    if field is None:
        u = [momentum[k] * over for k in range(3)]
    else:
        u = [(momentum[k] + 0.5 * field[k]) * over for k in range(3)]
    square = u[0] * u[0] + u[1] * u[1] + u[2] * u[2]
    base = omega * density * (1.0 - 1.5 * square)
    if field is not None:
        power = u[0] * field[0] + u[1] * field[1] + u[2] * field[2]
        base = base - (3.0 * factor) * power
    scaled = omega * density
    post = [None] * 19
    rest = (1.0 - omega) * f[0] + WEIGHTS[0] * base
    post[0] = jnp.where(wall, f[0], rest)
    for q in range(1, 19, 2):
        p = OPPOSITE[q]
        along = project(u, VELOCITY[q])
        flow = scaled * along
        inner = 4.5 * flow
        odd = 3.0 * flow
        if field is not None:
            pushed = project(field, VELOCITY[q])
            inner = inner + (9.0 * factor) * pushed
            odd = odd + (3.0 * factor) * pushed
        even = WEIGHTS[q] * (base + along * inner)
        odd = WEIGHTS[q] * odd
        post[q] = jnp.where(wall, f[p], (1.0 - omega) * f[q] + (even + odd))
        post[p] = jnp.where(wall, f[q], (1.0 - omega) * f[p] + (even - odd))
    return post


def kernel(
    sizes,
    pop, solid, mpos, moff, links, pcol,
    outf, outs,
    post, ysend, yhalo, zsend, zhalo, zin, mom, gfield, vsplit,
    msend, mrecv, disp, dback, where_to, terms, pz, plane,
    msend_sem, mrecv_sem, hsend_sem, hrecv_sem, bsend_sem, brecv_sem,
):
    nx, ny, nz, blocks, cap, cx = sizes
    slots = nx * cap
    gx, gy, gz = lax.axis_index("gx"), lax.axis_index("gy"), lax.axis_index("gz")
    right, left = lax.rem(gx + 1, nx), lax.rem(gx + nx - 1, nx)
    up, down = lax.rem(gy + 1, ny), lax.rem(gy + ny - 1, ny)
    other = lax.rem(gz + 1, nz)

    barrier = pltpu.get_barrier_semaphore()
    near = [(gx, up, gz), (gx, down, gz), (gx, gy, other)]
    near += [(a, b, gz) for a in (right, left) for b in (up, down)]
    near += [(right, gy, other), (left, gy, other), (gx, up, other), (gx, down, other)]
    for o in range(1, nx):
        near.append((lax.rem(gx + o, nx), gy, gz))
    for device in near:
        pl.semaphore_signal(barrier, inc=1, device_id=device, device_id_type=MESH)

    row = lax.broadcasted_iota(jnp.int32, (8, 128), 0)
    lane = lax.broadcasted_iota(jnp.int32, (8, 128), 1)

    columns = jnp.broadcast_to(pcol[...], (blocks, 128))
    named = [jnp.broadcast_to(columns[b : b + 1, :], (8, 128)) for b in range(blocks)]
    spots = []
    for b in range(blocks):
        spot = named[b] * cap
        for e in range(b):
            spot = spot + jnp.where(named[e] == named[b], 1, 0)
        spots.append(spot)
        where_to[b] = spot
    tiles = []
    for b in range(blocks):
        tiles.append(
            jnp.concatenate([mpos[b], moff[b], links[b].astype(jnp.float32)], axis=0)
        )
    empty = jnp.where(row < 3, PARK, 0.0)
    for s in range(slots):
        tile = empty
        for b in range(blocks):
            tile = jnp.where(spots[b] == s, tiles[b], tile)
        msend[s] = tile

    pl.semaphore_wait(barrier, len(near))

    def exchange(source, target, send_sem, recv_sem):
        copies = []
        for o in range(1, nx):
            to = lax.rem(gx + o, nx)
            copy = pltpu.make_async_remote_copy(
                src_ref=source.at[pl.ds(to * cap, cap)],
                dst_ref=target.at[pl.ds(gx * cap, cap)],
                send_sem=send_sem.at[o],
                recv_sem=recv_sem.at[o],
                device_id=(to, gy, gz),
                device_id_type=MESH,
            )
            copy.start()
            copies.append(copy)
        for k in range(cap):
            target[gx * cap + k] = source[gx * cap + k]
        return copies

    marker_copies = exchange(msend, mrecv, msend_sem, mrecv_sem)

    def halo(step):
        copies = []

        def go(source, target, device):
            n = len(copies)
            copy = pltpu.make_async_remote_copy(
                src_ref=source,
                dst_ref=target,
                send_sem=hsend_sem.at[step, n],
                recv_sem=hrecv_sem.at[step, n],
                device_id=device,
                device_id_type=MESH,
            )
            copy.start()
            copies.append(copy)

        z = zsend.at[step]
        go(z, zhalo.at[step, 1], (right, gy, other))
        go(z, zhalo.at[step, 2], (left, gy, other))
        go(z, zhalo.at[step, 3], (gx, up, other))
        go(z, zhalo.at[step, 4], (gx, down, other))
        for d, b in ((0, up), (1, down)):
            for j, x, a in ((1, cx - 1, right), (2, 0, left)):
                go(
                    ysend.at[step, d, j, pl.ds(x, 1)],
                    yhalo.at[step, d, j, pl.ds(cx, 1)],
                    (a, b, gz),
                )
        go(post.at[step, pl.ds(9, 5), cx], post.at[step, pl.ds(9, 5), 0], (right, gy, gz))
        go(post.at[step, pl.ds(14, 5), 1], post.at[step, pl.ds(14, 5), cx + 1], (left, gy, gz))
        go(ysend.at[step, 0], yhalo.at[step, 0, :, pl.ds(0, cx)], (gx, up, gz))
        go(ysend.at[step, 1], yhalo.at[step, 1, :, pl.ds(0, cx)], (gx, down, gz))
        go(z, zhalo.at[step, 0], (gx, gy, other))
        return copies

    def emit(step, x, values):
        for q in range(19):
            post[step, PLACE[q], x + 1] = values[q]

    def rim(step, x, values, packed):
        for d, edge in ((0, 7), (1, 0)):
            for j, q in enumerate(Y_MOVERS[d]):
                ysend[step, d, j, pl.ds(x, 1)] = values[q][edge : edge + 1, :]
        for d, edge in ((0, 127), (1, 0)):
            for j, q in enumerate(Z_MOVERS[d]):
                column = jnp.broadcast_to(values[q][:, edge : edge + 1], (8, 128))
                packed = jnp.where(lane == x + (d * HALF + j * 8), column, packed)
        return packed

    def stream(step, x, last):
        turned = pltpu.roll(zin[...], lax.rem(128 - x, 128), axis=1)
        f = []
        for q in range(19):
            c = VELOCITY[q]
            tile = post[step, PLACE[q], x + 1 - c[0]]
            if c[1]:
                d = 0 if c[1] == 1 else 1
                j = Y_MOVERS[d].index(q)
                if c[0] == 1:
                    at = lax.rem(x + cx, cx + 1)
                else:
                    at = x - c[0]
                line = jnp.broadcast_to(yhalo[step, d, j, pl.ds(at, 1)], (8, 128))
                tile = jnp.where(row == (0 if d == 0 else 7), line, pltpu.roll(tile, 1 if d == 0 else 7, axis=0))
            if c[2]:
                d = 0 if c[2] == 1 else 1
                j = Z_MOVERS[d].index(q)
                k = d * HALF + j * 8
                column = jnp.broadcast_to(turned[:, k : k + 1], (8, 128))
                tile = jnp.where(
                    lane == (0 if d == 0 else 127), column, pltpu.roll(tile, 1 if d == 0 else 127, axis=1)
                )
            f.append(tile)
            outf[q, x] = tile
        density, momentum = moments(f)
        mom[0, x] = density
        over = 1.0 / density
        for k in range(3):
            mom[k + 1, x] = momentum[k]
            v = momentum[k] * over
            gfield[k, x] = v

    def combine(step):
        face = zhalo[step, 0]
        group = lax.rem(lane, HALF) // 8
        inside = lax.rem(lane, 8)
        forward = jnp.where(
            inside == 0, pltpu.roll(zhalo[step, 1], 121, axis=1), pltpu.roll(face, 1, axis=1)
        )
        backward = jnp.where(
            inside == 7, pltpu.roll(zhalo[step, 2], 7, axis=1), pltpu.roll(face, 127, axis=1)
        )
        rising = jnp.where(
            row == 0, pltpu.roll(zhalo[step, 3], 1, axis=0), pltpu.roll(face, 1, axis=0)
        )
        falling = jnp.where(
            row == 7, pltpu.roll(zhalo[step, 4], 7, axis=0), pltpu.roll(face, 7, axis=0)
        )
        zin[...] = jnp.where(
            group == 0,
            face,
            jnp.where(
                group == 1,
                forward,
                jnp.where(group == 2, backward, jnp.where(group == 3, rising, falling)),
            ),
        )

    def spread(step):
        depth = lax.broadcasted_iota(jnp.int32, (128, 128), 0).astype(jnp.float32)
        cell = row.astype(jnp.float32)

        def one(s, carry):
            info = mrecv[s]
            if step == 0:
                shift = jnp.zeros((8, 128), jnp.float32)
                disp[s] = shift
            else:
                shift = disp[s]
            position = info + shift
            rest_to_anchor = pltpu.roll(info, 5, axis=0)
            force = K_TETHER * ((info + rest_to_anchor) - position)
            if step > 0:
                for k in range(2):
                    index = jnp.broadcast_to(info[6 + k : 7 + k, :], (8, 128)).astype(jnp.int32)
                    chosen = jnp.take_along_axis(shift, index, axis=1)
                    force = force + K_SPRING * (chosen - shift)
            at = pl.ds(pl.multiple_of(s * 128, 128), 128)
            wz = jnp.maximum(0.0, 1.0 - jnp.abs(position[2:3, :] - depth))
            high = wz.astype(jnp.bfloat16)
            pz[0:128, at] = high
            pz[128:256, at] = (wz - high.astype(jnp.float32)).astype(jnp.bfloat16)
            wx = jnp.maximum(0.0, 1.0 - jnp.abs(position[0:1, :] - cell))
            wy = jnp.maximum(0.0, 1.0 - jnp.abs(position[1:2, :] - cell))
            full = jnp.concatenate([wx[i : i + 1, :] * wy for i in range(8)], axis=0)
            plane[:, at] = full
            for k in range(3):
                term = force[k : k + 1, :] * full
                high = term.astype(jnp.bfloat16)
                terms[k * 64 : k * 64 + 64, at] = high
                terms[192 + k * 64 : 256 + k * 64, at] = (
                    term - high.astype(jnp.float32)
                ).astype(jnp.bfloat16)
            return carry

        lax.fori_loop(0, slots, one, 0)
        product = lax.dot_general(
            terms[...], pz[...], (((1,), (1,)), ((), ())), preferred_element_type=jnp.float32
        )
        total = product[0:192, 0:128] + (product[0:192, 128:256] + product[192:384, 0:128])
        gfield[...] = total.reshape(3, 8, 8, 128)

    def sample():
        v = gfield[...].reshape(192, 128)
        high = v.astype(jnp.bfloat16)
        low = (v - high.astype(jnp.float32)).astype(jnp.bfloat16)
        vsplit[0:192, 0:128] = high
        vsplit[0:192, 128:256] = high
        vsplit[192:384, 0:128] = low
        vsplit[192:384, 128:256] = low

        def pair(i, carry):
            at = pl.ds(pl.multiple_of(i * 256, 256), 256)
            product = jnp.dot(vsplit[...], pz[:, at], preferred_element_type=jnp.float32)
            full = plane[:, at]
            for k in range(3):
                part = (product[k * 64 : k * 64 + 64] + product[192 + k * 64 : 256 + k * 64]) * full
                moved = jnp.sum(part, axis=0, keepdims=True)
                for h in range(2):
                    disp[2 * i + h, k : k + 1, :] = (
                        disp[2 * i + h, k : k + 1, :] + moved[:, h * 128 : h * 128 + 128]
                    )
            return carry

        lax.fori_loop(0, slots // 2, pair, 0)

    def first(x, packed):
        f = [pop[q, x] for q in range(19)]
        density, momentum = moments(f)
        mom[0, x] = density
        for k in range(3):
            mom[k + 1, x] = momentum[k]
        values = collide(f, density, momentum, None, solid[x] == 1)
        emit(0, x, values)
        return rim(0, x, values, packed)

    zsend[0] = lax.fori_loop(0, cx, first, jnp.zeros((8, 128), jnp.float32))
    halos = [halo(0)]
    for copy in marker_copies:
        copy.wait_recv()
    spread(0)

    def driven(x, carry):
        f = [pop[q, x] for q in range(19)]
        values = collide(
            f, mom[0, x], [mom[k, x] for k in range(1, 4)], [gfield[k, x] for k in range(3)],
            solid[x] == 1,
        )
        emit(0, x, values)
        return carry

    lax.fori_loop(2, cx - 2, driven, 0)

    for step in range(STEPS):
        if step > 0:
            spread(step)

            def coupled(x, packed):
                f = [outf[q, x] for q in range(19)]
                values = collide(
                    f, mom[0, x], [mom[k, x] for k in range(1, 4)],
                    [gfield[k, x] for k in range(3)], solid[x] == 1,
                )
                emit(step, x, values)
                return rim(step, x, values, packed)

            zsend[step] = lax.fori_loop(0, cx, coupled, jnp.zeros((8, 128), jnp.float32))
            halos.append(halo(step))
        for copy in halos[step]:
            copy.wait_recv()
        combine(step)

        def moving(x, carry):
            stream(step, x, step == STEPS - 1)
            return carry

        lax.fori_loop(0, cx, moving, 0)
        sample()

    back_copies = exchange(disp, dback, bsend_sem, brecv_sem)
    for copy in back_copies:
        copy.wait_recv()
    for b in range(blocks):
        tile = jnp.zeros((8, 128), jnp.float32)
        spot = where_to[b]
        for s in range(slots):
            tile = jnp.where(spot == s, dback[s], tile)
        outs[b] = tile[0:3, :]
    for copies in [marker_copies] + halos + [back_copies]:
        for copy in copies:
            copy.wait_send()


def shards(sizes, populations, solid, marker_pos, anchor_offset, links, patch_col):
    nx, ny, nz, blocks, cap, cx = sizes
    slots = nx * cap
    f32 = jnp.float32
    tile = (8, 128)
    vmem = pl.BlockSpec(memory_space=pltpu.VMEM)
    dma = pltpu.SemaphoreType.DMA
    return pl.pallas_call(
        functools.partial(kernel, sizes),
        out_shape=(
            jax.ShapeDtypeStruct(populations.shape, f32),
            jax.ShapeDtypeStruct(marker_pos.shape, f32),
        ),
        in_specs=[vmem] * 6,
        out_specs=(vmem, vmem),
        scratch_shapes=[
            pltpu.VMEM((STEPS, 19, cx + 2) + tile, f32),
            pltpu.VMEM((STEPS, 2, 5) + tile, f32),
            pltpu.VMEM((STEPS, 2, 5, 16, 128), f32),
            pltpu.VMEM((STEPS,) + tile, f32),
            pltpu.VMEM((STEPS, 5) + tile, f32),
            pltpu.VMEM(tile, f32),
            pltpu.VMEM((4, cx) + tile, f32),
            pltpu.VMEM((3, cx) + tile, f32),
            pltpu.VMEM((384, 256), jnp.bfloat16),
            pltpu.VMEM((slots,) + tile, f32),
            pltpu.VMEM((slots,) + tile, f32),
            pltpu.VMEM((slots,) + tile, f32),
            pltpu.VMEM((slots,) + tile, f32),
            pltpu.VMEM((blocks,) + tile, jnp.int32),
            pltpu.VMEM((384, slots * 128), jnp.bfloat16),
            pltpu.VMEM((256, slots * 128), jnp.bfloat16),
            pltpu.VMEM((64, slots * 128), f32),
            dma((nx,)), dma((nx,)),
            dma((STEPS, 13)), dma((STEPS, 13)),
            dma((nx,)), dma((nx,)),
        ],
        compiler_params=pltpu.CompilerParams(
            collective_id=0, has_side_effects=True, vmem_limit_bytes=40 * 1024 * 1024
        ),
    )(populations, solid, marker_pos, anchor_offset, links, patch_col)


def solution(mesh):
    placed = (
        P(None, "gx", "gy", "gz"),
        P("gx", "gy", "gz"),
        P(("gx", "gy", "gz"), None, None),
        P(("gx", "gy", "gz"), None, None),
        P(("gx", "gy", "gz"), None, None),
        P(("gx", "gy", "gz"), None),
    )

    def whole(populations, solid, marker_pos, anchor_offset, links, patch_col):
        nx, ny, nz = (mesh.shape[name] for name in ("gx", "gy", "gz"))
        blocks = marker_pos.shape[0] // (nx * ny * nz)
        cap = max(2, 2 * blocks // nx)
        sizes = (nx, ny, nz, blocks, cap, populations.shape[1] // nx)
        return jax.shard_map(
            functools.partial(shards, sizes),
            mesh=mesh,
            in_specs=placed,
            out_specs=(P(None, "gx", "gy", "gz"), P(("gx", "gy", "gz"), None, None)),
            check_vma=False,
        )(populations, solid, marker_pos, anchor_offset, links, patch_col)

    return whole
```

```python
import functools

import jax
import jax.numpy as jnp
from jax import lax
from jax.experimental import pallas as pl
from jax.experimental.pallas import tpu as pltpu
from jax.sharding import PartitionSpec as P

STEPS = 3
VELOCITY = (
    (0, 0, 0), (1, 0, 0), (-1, 0, 0), (0, 1, 0), (0, -1, 0), (0, 0, 1), (0, 0, -1),
    (1, 1, 0), (-1, -1, 0), (1, -1, 0), (-1, 1, 0), (1, 0, 1), (-1, 0, -1), (1, 0, -1),
    (-1, 0, 1), (0, 1, 1), (0, -1, -1), (0, 1, -1), (0, -1, 1),
)
WEIGHTS = (1.0 / 3.0,) + (1.0 / 18.0,) * 6 + (1.0 / 36.0,) * 12
OPPOSITE = (0, 2, 1, 4, 3, 6, 5, 8, 7, 10, 9, 12, 11, 14, 13, 16, 15, 18, 17)
TAU = 0.8
K_TETHER = 0.05
K_SPRING = 0.1
NUMBER = {c: q for q, c in enumerate(VELOCITY)}
ORDER = (
    [q for q in range(19) if VELOCITY[q][0] == 0]
    + [q for q in range(19) if VELOCITY[q][0] == 1]
    + [q for q in range(19) if VELOCITY[q][0] == -1]
)
PLACE = {q: i for i, q in enumerate(ORDER)}
Y_MOVERS = [
    [NUMBER[(0, s, 0)], NUMBER[(1, s, 0)], NUMBER[(-1, s, 0)], NUMBER[(0, s, 1)], NUMBER[(0, s, -1)]]
    for s in (1, -1)
]
Z_MOVERS = [
    [NUMBER[(0, 0, s)], NUMBER[(1, 0, s)], NUMBER[(-1, 0, s)], NUMBER[(0, 1, s)], NUMBER[(0, -1, s)]]
    for s in (1, -1)
]
MESH = pl.DeviceIdType.MESH
PARK = -1000.0
SPREAD_UNROLL = 16
CELL_UNROLL = 8
WIDE = 1024
HALF = 64


def axis_sum(values, column):
    total = None
    for q in range(19):
        sign = VELOCITY[q][column]
        if sign == 0:
            continue
        term = values[q]
        total = (term if sign == 1 else -term) if total is None else (
            total + term if sign == 1 else total - term
        )
    return total


def moments(f):
    density = f[0]
    for q in range(1, 19):
        density = density + f[q]
    return density, [axis_sum(f, column) for column in range(3)]


def project(vector, direction):
    total = None
    for column in range(3):
        if direction[column]:
            term = vector[column] if direction[column] == 1 else -vector[column]
            total = term if total is None else total + term
    return total


def collide(f, density, momentum, field, wall):
    over = 1.0 / density
    omega = 1.0 / TAU
    factor = 1.0 - 0.5 / TAU
    if field is None:
        u = [momentum[k] * over for k in range(3)]
    else:
        u = [(momentum[k] + 0.5 * field[k]) * over for k in range(3)]
    square = u[0] * u[0] + u[1] * u[1] + u[2] * u[2]
    base = omega * density * (1.0 - 1.5 * square)
    if field is not None:
        power = u[0] * field[0] + u[1] * field[1] + u[2] * field[2]
        base = base - (3.0 * factor) * power
    scaled = omega * density
    post = [None] * 19
    rest = (1.0 - omega) * f[0] + WEIGHTS[0] * base
    post[0] = jnp.where(wall, f[0], rest)
    for q in range(1, 19, 2):
        p = OPPOSITE[q]
        along = project(u, VELOCITY[q])
        flow = scaled * along
        inner = 4.5 * flow
        odd = 3.0 * flow
        if field is not None:
            pushed = project(field, VELOCITY[q])
            inner = inner + (9.0 * factor) * pushed
            odd = odd + (3.0 * factor) * pushed
        even = WEIGHTS[q] * (base + along * inner)
        odd = WEIGHTS[q] * odd
        post[q] = jnp.where(wall, f[p], (1.0 - omega) * f[q] + (even + odd))
        post[p] = jnp.where(wall, f[q], (1.0 - omega) * f[p] + (even - odd))
    return post


def kernel(
    sizes,
    pop_hbm, solid, mpos, moff, links, pcol,
    outf, outs, pop,
    post, ysend, yhalo, zsend, zhalo, zin, mom, gfield, vsplit,
    msend, mrecv, disp, dback, where_to, terms, pz, plane,
    pop_sem, msend_sem, mrecv_sem, hsend_sem, hrecv_sem, bsend_sem, brecv_sem,
):
    nx, ny, nz, blocks, cap, cx = sizes
    slots = nx * cap
    gx, gy, gz = lax.axis_index("gx"), lax.axis_index("gy"), lax.axis_index("gz")
    right, left = lax.rem(gx + 1, nx), lax.rem(gx + nx - 1, nx)
    up, down = lax.rem(gy + 1, ny), lax.rem(gy + ny - 1, ny)
    other = lax.rem(gz + 1, nz)

    fetch = pltpu.make_async_copy(pop_hbm, pop, pop_sem)
    fetch.start()
    barrier = pltpu.get_barrier_semaphore()
    near = [(gx, up, gz), (gx, down, gz), (gx, gy, other)]
    near += [(a, b, gz) for a in (right, left) for b in (up, down)]
    near += [(right, gy, other), (left, gy, other), (gx, up, other), (gx, down, other)]
    for o in range(1, nx):
        near.append((lax.rem(gx + o, nx), gy, gz))
    for device in near:
        pl.semaphore_signal(barrier, inc=1, device_id=device, device_id_type=MESH)

    row = lax.broadcasted_iota(jnp.int32, (8, 128), 0)
    lane = lax.broadcasted_iota(jnp.int32, (8, 128), 1)

    named = [jnp.broadcast_to(pcol[:, b : b + 1], (8, 128)) for b in range(blocks)]
    spots = []
    for b in range(blocks):
        spot = named[b] * cap
        for e in range(b):
            spot = spot + jnp.where(named[e] == named[b], 1, 0)
        spots.append(spot)
        where_to[b] = spot
    tiles = []
    for b in range(blocks):
        tiles.append(
            jnp.concatenate(
                [mpos[k, b : b + 1, :] for k in range(3)]
                + [moff[k, b : b + 1, :] for k in range(3)]
                + [links[b].astype(jnp.float32)],
                axis=0,
            )
        )
    empty = jnp.where(row < 3, PARK, 0.0)
    for s in range(slots):
        tile = empty
        for b in range(blocks):
            tile = jnp.where(spots[b] == s, tiles[b], tile)
        msend[s] = tile

    pl.semaphore_wait(barrier, len(near))

    def exchange(source, target, send_sem, recv_sem):
        copies = []
        for o in range(1, nx):
            to = lax.rem(gx + o, nx)
            copy = pltpu.make_async_remote_copy(
                src_ref=source.at[pl.ds(to * cap, cap)],
                dst_ref=target.at[pl.ds(gx * cap, cap)],
                send_sem=send_sem.at[o],
                recv_sem=recv_sem.at[o],
                device_id=(to, gy, gz),
                device_id_type=MESH,
            )
            copy.start()
            copies.append(copy)
        for k in range(cap):
            target[gx * cap + k] = source[gx * cap + k]
        return copies

    marker_copies = exchange(msend, mrecv, msend_sem, mrecv_sem)

    def halo(step):
        copies = []

        def go(source, target, device):
            n = len(copies)
            copy = pltpu.make_async_remote_copy(
                src_ref=source,
                dst_ref=target,
                send_sem=hsend_sem.at[step, n],
                recv_sem=hrecv_sem.at[step, n],
                device_id=device,
                device_id_type=MESH,
            )
            copy.start()
            copies.append(copy)

        z = zsend.at[step]
        go(z, zhalo.at[step, 1], (right, gy, other))
        go(z, zhalo.at[step, 2], (left, gy, other))
        go(z, zhalo.at[step, 3], (gx, up, other))
        go(z, zhalo.at[step, 4], (gx, down, other))
        for d, b in ((0, up), (1, down)):
            for j, x, a in ((1, cx - 1, right), (2, 0, left)):
                go(
                    ysend.at[step, d, j, pl.ds(x, 1)],
                    yhalo.at[step, d, j, pl.ds(cx, 1)],
                    (a, b, gz),
                )
        go(post.at[step, pl.ds(9, 5), cx], post.at[step, pl.ds(9, 5), 0], (right, gy, gz))
        go(post.at[step, pl.ds(14, 5), 1], post.at[step, pl.ds(14, 5), cx + 1], (left, gy, gz))
        go(ysend.at[step, 0], yhalo.at[step, 0, :, pl.ds(0, cx)], (gx, up, gz))
        go(ysend.at[step, 1], yhalo.at[step, 1, :, pl.ds(0, cx)], (gx, down, gz))
        go(z, zhalo.at[step, 0], (gx, gy, other))
        return copies

    def emit(step, x, values):
        for q in range(19):
            post[step, PLACE[q], x + 1] = values[q]

    def rim(step, x, values, packed):
        for d, edge in ((0, 7), (1, 0)):
            for j, q in enumerate(Y_MOVERS[d]):
                ysend[step, d, j, pl.ds(x, 1)] = values[q][edge : edge + 1, :]
        for d, edge in ((0, 127), (1, 0)):
            for j, q in enumerate(Z_MOVERS[d]):
                column = jnp.broadcast_to(values[q][:, edge : edge + 1], (8, 128))
                packed = jnp.where(lane == x + (d * HALF + j * 8), column, packed)
        return packed

    def stream(step, x, last):
        turned = pltpu.roll(zin[...], lax.rem(128 - x, 128), axis=1)
        f = []
        for q in range(19):
            c = VELOCITY[q]
            tile = post[step, PLACE[q], x + 1 - c[0]]
            if c[1]:
                d = 0 if c[1] == 1 else 1
                j = Y_MOVERS[d].index(q)
                if c[0] == 1:
                    at = lax.rem(x + cx, cx + 1)
                else:
                    at = x - c[0]
                line = jnp.broadcast_to(yhalo[step, d, j, pl.ds(at, 1)], (8, 128))
                tile = jnp.where(row == (0 if d == 0 else 7), line, pltpu.roll(tile, 1 if d == 0 else 7, axis=0))
            if c[2]:
                d = 0 if c[2] == 1 else 1
                j = Z_MOVERS[d].index(q)
                k = d * HALF + j * 8
                column = jnp.broadcast_to(turned[:, k : k + 1], (8, 128))
                tile = jnp.where(
                    lane == (0 if d == 0 else 127), column, pltpu.roll(tile, 1 if d == 0 else 127, axis=1)
                )
            f.append(tile)
            outf[q, x] = tile
        density, momentum = moments(f)
        mom[0, x] = density
        over = 1.0 / density
        for k in range(3):
            mom[k + 1, x] = momentum[k]
            v = momentum[k] * over
            gfield[k, x] = v

    def combine(step):
        face = zhalo[step, 0]
        group = lax.rem(lane, HALF) // 8
        inside = lax.rem(lane, 8)
        forward = jnp.where(
            inside == 0, pltpu.roll(zhalo[step, 1], 121, axis=1), pltpu.roll(face, 1, axis=1)
        )
        backward = jnp.where(
            inside == 7, pltpu.roll(zhalo[step, 2], 7, axis=1), pltpu.roll(face, 127, axis=1)
        )
        rising = jnp.where(
            row == 0, pltpu.roll(zhalo[step, 3], 1, axis=0), pltpu.roll(face, 1, axis=0)
        )
        falling = jnp.where(
            row == 7, pltpu.roll(zhalo[step, 4], 7, axis=0), pltpu.roll(face, 7, axis=0)
        )
        zin[...] = jnp.where(
            group == 0,
            face,
            jnp.where(
                group == 1,
                forward,
                jnp.where(group == 2, backward, jnp.where(group == 3, rising, falling)),
            ),
        )

    def reach(step):
        return (2, cx - 2) if step == 0 else (0, cx)

    def spread(step):
        x0, x1 = reach(step)
        size = (x1 - x0) * 8
        n = 3 * size
        depth = lax.broadcasted_iota(jnp.int32, (128, 128), 0).astype(jnp.float32)
        cell = row.astype(jnp.float32)

        def one(s, carry):
            info = mrecv[s]
            if step == 0:
                shift = jnp.zeros((8, 128), jnp.float32)
                disp[s] = shift
            else:
                shift = disp[s]
            position = info + shift
            rest_to_anchor = pltpu.roll(info, 5, axis=0)
            force = K_TETHER * ((info + rest_to_anchor) - position)
            if step > 0:
                for k in range(2):
                    index = jnp.broadcast_to(info[6 + k : 7 + k, :], (8, 128)).astype(jnp.int32)
                    chosen = jnp.take_along_axis(shift, index, axis=1)
                    force = force + K_SPRING * (chosen - shift)
            at = pl.ds(pl.multiple_of(s * 128, 128), 128)
            wz = jnp.maximum(0.0, 1.0 - jnp.abs(position[2:3, :] - depth))
            high = wz.astype(jnp.bfloat16)
            pz[0:128, at] = high
            pz[128:256, at] = (wz - high.astype(jnp.float32)).astype(jnp.bfloat16)
            wx = jnp.maximum(0.0, 1.0 - jnp.abs(position[0:1, :] - cell))
            wy = jnp.maximum(0.0, 1.0 - jnp.abs(position[1:2, :] - cell))
            full = jnp.concatenate([wx[i : i + 1, :] * wy for i in range(x0, x1)], axis=0)
            plane[0:size, at] = full
            for k in range(3):
                term = force[k : k + 1, :] * full
                high = term.astype(jnp.bfloat16)
                terms[k * size : k * size + size, at] = high
                terms[n + k * size : n + k * size + size, at] = (
                    term - high.astype(jnp.float32)
                ).astype(jnp.bfloat16)
            return carry

        lax.fori_loop(0, slots, one, 0, unroll=SPREAD_UNROLL)
        product = lax.dot_general(
            terms[0 : 2 * n], pz[...], (((1,), (1,)), ((), ())), preferred_element_type=jnp.float32
        )
        total = product[0:n, 0:128] + (product[0:n, 128:256] + product[n : 2 * n, 0:128])
        gfield[:, x0:x1] = total.reshape(3, x1 - x0, 8, 128)

    def sample(step):
        x0, x1 = reach(step)
        size = (x1 - x0) * 8
        n = 3 * size
        v = gfield[:, x0:x1].reshape(n, 128)
        high = v.astype(jnp.bfloat16)
        low = (v - high.astype(jnp.float32)).astype(jnp.bfloat16)
        vsplit[0:n, 0:128] = high
        vsplit[0:n, 128:256] = high
        vsplit[n : 2 * n, 0:128] = low
        vsplit[n : 2 * n, 128:256] = low
        for i in range(slots * 128 // WIDE):
            at = pl.ds(i * WIDE, WIDE)
            product = jnp.dot(vsplit[0 : 2 * n], pz[:, at], preferred_element_type=jnp.float32)
            full = plane[0:size, at]
            for k in range(3):
                part = product[k * size : k * size + size] + product[n + k * size : n + k * size + size]
                moved = jnp.sum(part * full, axis=0, keepdims=True)
                for h in range(WIDE // 128):
                    slot = i * (WIDE // 128) + h
                    disp[slot, k : k + 1, :] = (
                        disp[slot, k : k + 1, :] + moved[:, h * 128 : h * 128 + 128]
                    )

    def first(x, packed):
        f = [pop[q, x] for q in range(19)]
        density, momentum = moments(f)
        mom[0, x] = density
        for k in range(3):
            mom[k + 1, x] = momentum[k]
        values = collide(f, density, momentum, None, solid[x] == 1)
        emit(0, x, values)
        return rim(0, x, values, packed)

    fetch.wait()
    zsend[0] = lax.fori_loop(0, cx, first, jnp.zeros((8, 128), jnp.float32), unroll=CELL_UNROLL)
    halos = [halo(0)]
    for copy in marker_copies:
        copy.wait_recv()
    spread(0)

    def driven(x, carry):
        f = [pop[q, x] for q in range(19)]
        values = collide(
            f, mom[0, x], [mom[k, x] for k in range(1, 4)], [gfield[k, x] for k in range(3)],
            solid[x] == 1,
        )
        emit(0, x, values)
        return carry

    lax.fori_loop(2, cx - 2, driven, 0, unroll=CELL_UNROLL)

    for step in range(STEPS):
        if step > 0:
            spread(step)

            def coupled(x, packed):
                f = [outf[q, x] for q in range(19)]
                values = collide(
                    f, mom[0, x], [mom[k, x] for k in range(1, 4)],
                    [gfield[k, x] for k in range(3)], solid[x] == 1,
                )
                emit(step, x, values)
                return rim(step, x, values, packed)

            zsend[step] = lax.fori_loop(0, cx, coupled, jnp.zeros((8, 128), jnp.float32), unroll=CELL_UNROLL)
            halos.append(halo(step))
        for copy in halos[step]:
            copy.wait_recv()
        combine(step)

        def moving(x, carry):
            stream(step, x, step == STEPS - 1)
            return carry

        lax.fori_loop(0, cx, moving, 0, unroll=CELL_UNROLL)
        sample(step)

    back_copies = exchange(disp, dback, bsend_sem, brecv_sem)
    for copy in back_copies:
        copy.wait_recv()
    for b in range(blocks):
        tile = jnp.zeros((8, 128), jnp.float32)
        spot = where_to[b]
        for s in range(slots):
            tile = jnp.where(spot == s, dback[s], tile)
        for k in range(3):
            outs[k, b : b + 1, :] = tile[k : k + 1, :]
    for copies in [marker_copies] + halos + [back_copies]:
        for copy in copies:
            copy.wait_send()


def shards(sizes, populations, solid, marker_pos, anchor_offset, links, patch_col):
    nx, ny, nz, blocks, cap, cx = sizes
    slots = nx * cap
    f32 = jnp.float32
    tile = (8, 128)
    vmem = pl.BlockSpec(memory_space=pltpu.VMEM)
    dma = pltpu.SemaphoreType.DMA
    new, shift = pl.pallas_call(
        functools.partial(kernel, sizes),
        out_shape=(
            jax.ShapeDtypeStruct(populations.shape, f32),
            jax.ShapeDtypeStruct((3, blocks, 128), f32),
        ),
        in_specs=[pl.BlockSpec(memory_space=pltpu.HBM)] + [vmem] * 5,
        out_specs=(vmem, vmem),
        scratch_shapes=[
            pltpu.VMEM(populations.shape, f32),
            pltpu.VMEM((STEPS, 19, cx + 2) + tile, f32),
            pltpu.VMEM((STEPS, 2, 5) + tile, f32),
            pltpu.VMEM((STEPS, 2, 5, 16, 128), f32),
            pltpu.VMEM((STEPS,) + tile, f32),
            pltpu.VMEM((STEPS, 5) + tile, f32),
            pltpu.VMEM(tile, f32),
            pltpu.VMEM((4, cx) + tile, f32),
            pltpu.VMEM((3, cx) + tile, f32),
            pltpu.VMEM((384, 256), jnp.bfloat16),
            pltpu.VMEM((slots,) + tile, f32),
            pltpu.VMEM((slots,) + tile, f32),
            pltpu.VMEM((slots,) + tile, f32),
            pltpu.VMEM((slots,) + tile, f32),
            pltpu.VMEM((blocks,) + tile, jnp.int32),
            pltpu.VMEM((384, slots * 128), jnp.bfloat16),
            pltpu.VMEM((256, slots * 128), jnp.bfloat16),
            pltpu.VMEM((64, slots * 128), f32),
            dma,
            dma((nx,)), dma((nx,)),
            dma((STEPS, 13)), dma((STEPS, 13)),
            dma((nx,)), dma((nx,)),
        ],
        compiler_params=pltpu.CompilerParams(
            collective_id=0, has_side_effects=True, vmem_limit_bytes=62 * 1024 * 1024
        ),
    )(
        populations,
        solid,
        jnp.transpose(marker_pos, (1, 0, 2)),
        jnp.transpose(anchor_offset, (1, 0, 2)),
        links,
        patch_col.T,
    )
    return new, jnp.transpose(shift, (1, 0, 2))


def solution(mesh):
    placed = (
        P(None, "gx", "gy", "gz"),
        P("gx", "gy", "gz"),
        P(("gx", "gy", "gz"), None, None),
        P(("gx", "gy", "gz"), None, None),
        P(("gx", "gy", "gz"), None, None),
        P(("gx", "gy", "gz"), None),
    )

    def whole(populations, solid, marker_pos, anchor_offset, links, patch_col):
        nx, ny, nz = (mesh.shape[name] for name in ("gx", "gy", "gz"))
        blocks = marker_pos.shape[0] // (nx * ny * nz)
        cap = max(2, 2 * blocks // nx)
        sizes = (nx, ny, nz, blocks, cap, populations.shape[1] // nx)
        return jax.shard_map(
            functools.partial(shards, sizes),
            mesh=mesh,
            in_specs=placed,
            out_specs=(P(None, "gx", "gy", "gz"), P(("gx", "gy", "gz"), None, None)),
            check_vma=False,
        )(populations, solid, marker_pos, anchor_offset, links, patch_col)

    return whole
```

```python
import functools

import jax
import jax.numpy as jnp
from jax import lax
from jax.experimental import pallas as pl
from jax.experimental.pallas import tpu as pltpu
from jax.sharding import PartitionSpec as P

STEPS = 3
VELOCITY = (
    (0, 0, 0), (1, 0, 0), (-1, 0, 0), (0, 1, 0), (0, -1, 0), (0, 0, 1), (0, 0, -1),
    (1, 1, 0), (-1, -1, 0), (1, -1, 0), (-1, 1, 0), (1, 0, 1), (-1, 0, -1), (1, 0, -1),
    (-1, 0, 1), (0, 1, 1), (0, -1, -1), (0, 1, -1), (0, -1, 1),
)
WEIGHTS = (1.0 / 3.0,) + (1.0 / 18.0,) * 6 + (1.0 / 36.0,) * 12
OPPOSITE = (0, 2, 1, 4, 3, 6, 5, 8, 7, 10, 9, 12, 11, 14, 13, 16, 15, 18, 17)
TAU = 0.8
K_TETHER = 0.05
K_SPRING = 0.1
NUMBER = {c: q for q, c in enumerate(VELOCITY)}
ORDER = (
    [q for q in range(19) if VELOCITY[q][0] == 0]
    + [q for q in range(19) if VELOCITY[q][0] == 1]
    + [q for q in range(19) if VELOCITY[q][0] == -1]
)
PLACE = {q: i for i, q in enumerate(ORDER)}
Y_MOVERS = [
    [NUMBER[(0, s, 0)], NUMBER[(1, s, 0)], NUMBER[(-1, s, 0)], NUMBER[(0, s, 1)], NUMBER[(0, s, -1)]]
    for s in (1, -1)
]
Z_MOVERS = [
    [NUMBER[(0, 0, s)], NUMBER[(1, 0, s)], NUMBER[(-1, 0, s)], NUMBER[(0, 1, s)], NUMBER[(0, -1, s)]]
    for s in (1, -1)
]
MESH = pl.DeviceIdType.MESH
PARK = -1000.0
SPREAD_UNROLL = 16
CELL_UNROLL = 8
WIDE = 1024
HALF = 64


def axis_sum(values, column):
    total = None
    for q in range(19):
        sign = VELOCITY[q][column]
        if sign == 0:
            continue
        term = values[q]
        total = (term if sign == 1 else -term) if total is None else (
            total + term if sign == 1 else total - term
        )
    return total


def moments(f):
    density = f[0]
    for q in range(1, 19):
        density = density + f[q]
    return density, [axis_sum(f, column) for column in range(3)]


def project(vector, direction):
    total = None
    for column in range(3):
        if direction[column]:
            term = vector[column] if direction[column] == 1 else -vector[column]
            total = term if total is None else total + term
    return total


def collide(f, density, momentum, field, wall):
    over = 1.0 / density
    omega = 1.0 / TAU
    factor = 1.0 - 0.5 / TAU
    if field is None:
        u = [momentum[k] * over for k in range(3)]
    else:
        u = [(momentum[k] + 0.5 * field[k]) * over for k in range(3)]
    square = u[0] * u[0] + u[1] * u[1] + u[2] * u[2]
    base = omega * density * (1.0 - 1.5 * square)
    if field is not None:
        power = u[0] * field[0] + u[1] * field[1] + u[2] * field[2]
        base = base - (3.0 * factor) * power
    scaled = omega * density
    post = [None] * 19
    rest = (1.0 - omega) * f[0] + WEIGHTS[0] * base
    post[0] = jnp.where(wall, f[0], rest)
    for q in range(1, 19, 2):
        p = OPPOSITE[q]
        along = project(u, VELOCITY[q])
        flow = scaled * along
        inner = 4.5 * flow
        odd = 3.0 * flow
        if field is not None:
            pushed = project(field, VELOCITY[q])
            inner = inner + (9.0 * factor) * pushed
            odd = odd + (3.0 * factor) * pushed
        even = WEIGHTS[q] * (base + along * inner)
        odd = WEIGHTS[q] * odd
        post[q] = jnp.where(wall, f[p], (1.0 - omega) * f[q] + (even + odd))
        post[p] = jnp.where(wall, f[q], (1.0 - omega) * f[p] + (even - odd))
    return post


def kernel(
    sizes,
    pop_hbm, solid, mpos, moff, links, pcol,
    outf, outs, pop,
    post, ysend, yhalo, zsend, zhalo, zin, mom, gfield, vsplit,
    msend, mrecv, disp, dsend, dback, where_to, terms, pz, plane,
    pop_sem, msend_sem, mrecv_sem, hsend_sem, hrecv_sem, bsend_sem, brecv_sem,
):
    nx, ny, nz, blocks, cap, cx = sizes
    slots = nx * cap
    gx, gy, gz = lax.axis_index("gx"), lax.axis_index("gy"), lax.axis_index("gz")
    right, left = lax.rem(gx + 1, nx), lax.rem(gx + nx - 1, nx)
    up, down = lax.rem(gy + 1, ny), lax.rem(gy + ny - 1, ny)
    other = lax.rem(gz + 1, nz)

    fetch = pltpu.make_async_copy(pop_hbm, pop, pop_sem)
    fetch.start()
    barrier = pltpu.get_barrier_semaphore()
    near = [(gx, up, gz), (gx, down, gz), (gx, gy, other)]
    near += [(a, b, gz) for a in (right, left) for b in (up, down)]
    near += [(right, gy, other), (left, gy, other), (gx, up, other), (gx, down, other)]
    for o in range(1, nx):
        near.append((lax.rem(gx + o, nx), gy, gz))
    for device in near:
        pl.semaphore_signal(barrier, inc=1, device_id=device, device_id_type=MESH)

    row = lax.broadcasted_iota(jnp.int32, (8, 128), 0)
    lane = lax.broadcasted_iota(jnp.int32, (8, 128), 1)

    named = [jnp.broadcast_to(pcol[:, b : b + 1], (8, 128)) for b in range(blocks)]
    spots = []
    for b in range(blocks):
        spot = named[b] * cap
        for e in range(b):
            spot = spot + jnp.where(named[e] == named[b], 1, 0)
        spots.append(spot)
        where_to[b] = spot
    tiles = []
    for b in range(blocks):
        tiles.append(
            jnp.concatenate(
                [mpos[k, b : b + 1, :] for k in range(3)]
                + [moff[k, b : b + 1, :] for k in range(3)]
                + [links[b].astype(jnp.float32)],
                axis=0,
            )
        )
    empty = jnp.where(row < 3, PARK, 0.0)
    for s in range(slots):
        tile = empty
        for b in range(blocks):
            tile = jnp.where(spots[b] == s, tiles[b], tile)
        msend[s] = tile

    pl.semaphore_wait(barrier, len(near))

    def exchange(source, target, count, send_sem, recv_sem):
        copies = []
        for o in range(1, nx):
            to = lax.rem(gx + o, nx)
            copy = pltpu.make_async_remote_copy(
                src_ref=source.at[pl.ds(to * count, count)],
                dst_ref=target.at[pl.ds(gx * count, count)],
                send_sem=send_sem.at[o],
                recv_sem=recv_sem.at[o],
                device_id=(to, gy, gz),
                device_id_type=MESH,
            )
            copy.start()
            copies.append(copy)
        for k in range(count):
            target[gx * count + k] = source[gx * count + k]
        return copies

    marker_copies = exchange(msend, mrecv, cap, msend_sem, mrecv_sem)

    def halo(step):
        copies = []

        def go(source, target, device):
            n = len(copies)
            copy = pltpu.make_async_remote_copy(
                src_ref=source,
                dst_ref=target,
                send_sem=hsend_sem.at[step, n],
                recv_sem=hrecv_sem.at[step, n],
                device_id=device,
                device_id_type=MESH,
            )
            copy.start()
            copies.append(copy)

        z = zsend.at[step]
        go(z, zhalo.at[step, 1], (right, gy, other))
        go(z, zhalo.at[step, 2], (left, gy, other))
        go(z, zhalo.at[step, 3], (gx, up, other))
        go(z, zhalo.at[step, 4], (gx, down, other))
        for d, b in ((0, up), (1, down)):
            for j, x, a in ((1, cx - 1, right), (2, 0, left)):
                go(
                    ysend.at[step, d, j, pl.ds(x, 1)],
                    yhalo.at[step, d, j, pl.ds(cx, 1)],
                    (a, b, gz),
                )
        go(post.at[step, pl.ds(9, 5), cx], post.at[step, pl.ds(9, 5), 0], (right, gy, gz))
        go(post.at[step, pl.ds(14, 5), 1], post.at[step, pl.ds(14, 5), cx + 1], (left, gy, gz))
        go(ysend.at[step, 0], yhalo.at[step, 0, :, pl.ds(0, cx)], (gx, up, gz))
        go(ysend.at[step, 1], yhalo.at[step, 1, :, pl.ds(0, cx)], (gx, down, gz))
        go(z, zhalo.at[step, 0], (gx, gy, other))
        return copies

    def emit(step, x, values):
        for q in range(19):
            post[step, PLACE[q], x + 1] = values[q]

    def rim(step, x, values, packed):
        for d, edge in ((0, 7), (1, 0)):
            for j, q in enumerate(Y_MOVERS[d]):
                ysend[step, d, j, pl.ds(x, 1)] = values[q][edge : edge + 1, :]
        for d, edge in ((0, 127), (1, 0)):
            for j, q in enumerate(Z_MOVERS[d]):
                column = jnp.broadcast_to(values[q][:, edge : edge + 1], (8, 128))
                packed = jnp.where(lane == x + (d * HALF + j * 8), column, packed)
        return packed

    def stream(step, x, last):
        turned = pltpu.roll(zin[...], lax.rem(128 - x, 128), axis=1)
        f = []
        for q in range(19):
            c = VELOCITY[q]
            tile = post[step, PLACE[q], x + 1 - c[0]]
            if c[1]:
                d = 0 if c[1] == 1 else 1
                j = Y_MOVERS[d].index(q)
                if c[0] == 1:
                    at = lax.rem(x + cx, cx + 1)
                else:
                    at = x - c[0]
                line = jnp.broadcast_to(yhalo[step, d, j, pl.ds(at, 1)], (8, 128))
                tile = jnp.where(row == (0 if d == 0 else 7), line, pltpu.roll(tile, 1 if d == 0 else 7, axis=0))
            if c[2]:
                d = 0 if c[2] == 1 else 1
                j = Z_MOVERS[d].index(q)
                k = d * HALF + j * 8
                column = jnp.broadcast_to(turned[:, k : k + 1], (8, 128))
                tile = jnp.where(
                    lane == (0 if d == 0 else 127), column, pltpu.roll(tile, 1 if d == 0 else 127, axis=1)
                )
            f.append(tile)
            outf[q, x] = tile
        density, momentum = moments(f)
        mom[0, x] = density
        over = 1.0 / density
        for k in range(3):
            mom[k + 1, x] = momentum[k]
            v = momentum[k] * over
            gfield[k, x] = v

    def combine(step):
        face = zhalo[step, 0]
        group = lax.rem(lane, HALF) // 8
        inside = lax.rem(lane, 8)
        forward = jnp.where(
            inside == 0, pltpu.roll(zhalo[step, 1], 121, axis=1), pltpu.roll(face, 1, axis=1)
        )
        backward = jnp.where(
            inside == 7, pltpu.roll(zhalo[step, 2], 7, axis=1), pltpu.roll(face, 127, axis=1)
        )
        rising = jnp.where(
            row == 0, pltpu.roll(zhalo[step, 3], 1, axis=0), pltpu.roll(face, 1, axis=0)
        )
        falling = jnp.where(
            row == 7, pltpu.roll(zhalo[step, 4], 7, axis=0), pltpu.roll(face, 7, axis=0)
        )
        zin[...] = jnp.where(
            group == 0,
            face,
            jnp.where(
                group == 1,
                forward,
                jnp.where(group == 2, backward, jnp.where(group == 3, rising, falling)),
            ),
        )

    def reach(step):
        return (2, cx - 2) if step == 0 else (0, cx)

    def spread(step):
        x0, x1 = reach(step)
        size = (x1 - x0) * 8
        n = 3 * size
        depth = lax.broadcasted_iota(jnp.int32, (128, 128), 0).astype(jnp.float32)
        cell = row.astype(jnp.float32)

        def one(s, carry):
            info = mrecv[s]
            if step == 0:
                shift = jnp.zeros((8, 128), jnp.float32)
                disp[s] = shift
            else:
                shift = disp[s]
            position = info + shift
            rest_to_anchor = pltpu.roll(info, 5, axis=0)
            force = K_TETHER * ((info + rest_to_anchor) - position)
            if step > 0:
                for k in range(2):
                    index = jnp.broadcast_to(info[6 + k : 7 + k, :], (8, 128)).astype(jnp.int32)
                    chosen = jnp.take_along_axis(shift, index, axis=1)
                    force = force + K_SPRING * (chosen - shift)
            at = pl.ds(pl.multiple_of(s * 128, 128), 128)
            wz = jnp.maximum(0.0, 1.0 - jnp.abs(position[2:3, :] - depth))
            high = wz.astype(jnp.bfloat16)
            pz[0:128, at] = high
            pz[128:256, at] = (wz - high.astype(jnp.float32)).astype(jnp.bfloat16)
            wx = jnp.maximum(0.0, 1.0 - jnp.abs(position[0:1, :] - cell))
            wy = jnp.maximum(0.0, 1.0 - jnp.abs(position[1:2, :] - cell))
            full = jnp.concatenate([wx[i : i + 1, :] * wy for i in range(x0, x1)], axis=0)
            plane[0:size, at] = full
            for k in range(3):
                term = force[k : k + 1, :] * full
                high = term.astype(jnp.bfloat16)
                terms[k * size : k * size + size, at] = high
                terms[n + k * size : n + k * size + size, at] = (
                    term - high.astype(jnp.float32)
                ).astype(jnp.bfloat16)
            return carry

        lax.fori_loop(0, slots, one, 0, unroll=SPREAD_UNROLL)
        product = lax.dot_general(
            terms[0 : 2 * n], pz[...], (((1,), (1,)), ((), ())), preferred_element_type=jnp.float32
        )
        total = product[0:n, 0:128] + (product[0:n, 128:256] + product[n : 2 * n, 0:128])
        gfield[:, x0:x1] = total.reshape(3, x1 - x0, 8, 128)

    def sample(step):
        x0, x1 = reach(step)
        size = (x1 - x0) * 8
        n = 3 * size
        v = gfield[:, x0:x1].reshape(n, 128)
        high = v.astype(jnp.bfloat16)
        low = (v - high.astype(jnp.float32)).astype(jnp.bfloat16)
        vsplit[0:n, 0:128] = high
        vsplit[0:n, 128:256] = high
        vsplit[n : 2 * n, 0:128] = low
        vsplit[n : 2 * n, 128:256] = low
        for i in range(slots * 128 // WIDE):
            at = pl.ds(i * WIDE, WIDE)
            product = jnp.dot(vsplit[0 : 2 * n], pz[:, at], preferred_element_type=jnp.float32)
            full = plane[0:size, at]
            for k in range(3):
                part = product[k * size : k * size + size] + product[n + k * size : n + k * size + size]
                moved = jnp.sum(part * full, axis=0, keepdims=True)
                for h in range(WIDE // 128):
                    slot = i * (WIDE // 128) + h
                    disp[slot, k : k + 1, :] = (
                        disp[slot, k : k + 1, :] + moved[:, h * 128 : h * 128 + 128]
                    )

    def first(x, packed):
        f = [pop[q, x] for q in range(19)]
        density, momentum = moments(f)
        mom[0, x] = density
        for k in range(3):
            mom[k + 1, x] = momentum[k]
        values = collide(f, density, momentum, None, solid[x] == 1)
        emit(0, x, values)
        return rim(0, x, values, packed)

    fetch.wait()
    zsend[0] = lax.fori_loop(0, cx, first, jnp.zeros((8, 128), jnp.float32), unroll=CELL_UNROLL)
    halos = [halo(0)]
    for copy in marker_copies:
        copy.wait_recv()
    spread(0)

    def driven(x, carry):
        f = [pop[q, x] for q in range(19)]
        values = collide(
            f, mom[0, x], [mom[k, x] for k in range(1, 4)], [gfield[k, x] for k in range(3)],
            solid[x] == 1,
        )
        emit(0, x, values)
        return carry

    lax.fori_loop(2, cx - 2, driven, 0, unroll=CELL_UNROLL)

    for step in range(STEPS):
        if step > 0:
            spread(step)

            def coupled(x, packed):
                f = [outf[q, x] for q in range(19)]
                values = collide(
                    f, mom[0, x], [mom[k, x] for k in range(1, 4)],
                    [gfield[k, x] for k in range(3)], solid[x] == 1,
                )
                emit(step, x, values)
                return rim(step, x, values, packed)

            zsend[step] = lax.fori_loop(0, cx, coupled, jnp.zeros((8, 128), jnp.float32), unroll=CELL_UNROLL)
            halos.append(halo(step))
        for copy in halos[step]:
            copy.wait_recv()
        combine(step)

        def moving(x, carry):
            stream(step, x, step == STEPS - 1)
            return carry

        lax.fori_loop(0, cx, moving, 0, unroll=CELL_UNROLL)
        sample(step)

    for i in range(slots // 2):
        dsend[i] = disp[2 * i] + pltpu.roll(disp[2 * i + 1], 4, axis=0)
    back_copies = exchange(dsend, dback, cap // 2, bsend_sem, brecv_sem)
    for copy in back_copies:
        copy.wait_recv()
    for b in range(blocks):
        tile = jnp.zeros((8, 128), jnp.float32)
        half = jnp.zeros((8, 128), jnp.float32)
        spot = where_to[b]
        for i in range(slots // 2):
            pair = dback[i]
            tile = jnp.where(spot == 2 * i, pair, tile)
            half = jnp.where(spot == 2 * i + 1, pair, half)
        tile = tile + pltpu.roll(half, 4, axis=0)
        for k in range(3):
            outs[k, b : b + 1, :] = tile[k : k + 1, :]
    for copies in [marker_copies] + halos + [back_copies]:
        for copy in copies:
            copy.wait_send()


def shards(sizes, populations, solid, marker_pos, anchor_offset, links, patch_col):
    nx, ny, nz, blocks, cap, cx = sizes
    slots = nx * cap
    f32 = jnp.float32
    tile = (8, 128)
    vmem = pl.BlockSpec(memory_space=pltpu.VMEM)
    dma = pltpu.SemaphoreType.DMA
    new, shift = pl.pallas_call(
        functools.partial(kernel, sizes),
        out_shape=(
            jax.ShapeDtypeStruct(populations.shape, f32),
            jax.ShapeDtypeStruct((3, blocks, 128), f32),
        ),
        in_specs=[pl.BlockSpec(memory_space=pltpu.HBM)] + [vmem] * 5,
        out_specs=(vmem, vmem),
        scratch_shapes=[
            pltpu.VMEM(populations.shape, f32),
            pltpu.VMEM((STEPS, 19, cx + 2) + tile, f32),
            pltpu.VMEM((STEPS, 2, 5) + tile, f32),
            pltpu.VMEM((STEPS, 2, 5, 16, 128), f32),
            pltpu.VMEM((STEPS,) + tile, f32),
            pltpu.VMEM((STEPS, 5) + tile, f32),
            pltpu.VMEM(tile, f32),
            pltpu.VMEM((4, cx) + tile, f32),
            pltpu.VMEM((3, cx) + tile, f32),
            pltpu.VMEM((384, 256), jnp.bfloat16),
            pltpu.VMEM((slots,) + tile, f32),
            pltpu.VMEM((slots,) + tile, f32),
            pltpu.VMEM((slots,) + tile, f32),
            pltpu.VMEM((slots // 2,) + tile, f32),
            pltpu.VMEM((slots // 2,) + tile, f32),
            pltpu.VMEM((blocks,) + tile, jnp.int32),
            pltpu.VMEM((384, slots * 128), jnp.bfloat16),
            pltpu.VMEM((256, slots * 128), jnp.bfloat16),
            pltpu.VMEM((64, slots * 128), f32),
            dma,
            dma((nx,)), dma((nx,)),
            dma((STEPS, 13)), dma((STEPS, 13)),
            dma((nx,)), dma((nx,)),
        ],
        compiler_params=pltpu.CompilerParams(
            collective_id=0, has_side_effects=True, vmem_limit_bytes=62 * 1024 * 1024
        ),
    )(
        populations,
        solid,
        jnp.transpose(marker_pos, (1, 0, 2)),
        jnp.transpose(anchor_offset, (1, 0, 2)),
        links,
        patch_col.T,
    )
    return new, jnp.transpose(shift, (1, 0, 2))


def solution(mesh):
    placed = (
        P(None, "gx", "gy", "gz"),
        P("gx", "gy", "gz"),
        P(("gx", "gy", "gz"), None, None),
        P(("gx", "gy", "gz"), None, None),
        P(("gx", "gy", "gz"), None, None),
        P(("gx", "gy", "gz"), None),
    )

    def whole(populations, solid, marker_pos, anchor_offset, links, patch_col):
        nx, ny, nz = (mesh.shape[name] for name in ("gx", "gy", "gz"))
        blocks = marker_pos.shape[0] // (nx * ny * nz)
        cap = max(2, 2 * blocks // nx)
        sizes = (nx, ny, nz, blocks, cap, populations.shape[1] // nx)
        return jax.shard_map(
            functools.partial(shards, sizes),
            mesh=mesh,
            in_specs=placed,
            out_specs=(P(None, "gx", "gy", "gz"), P(("gx", "gy", "gz"), None, None)),
            check_vma=False,
        )(populations, solid, marker_pos, anchor_offset, links, patch_col)

    return whole
```
